512 devices in a mesh: gx: 64 (over z, x_hi, core), col: 8 (over y, x_lo).
Axes of the slice: x: 4 (x_hi: 2, x_lo: 2; x = x_hi * 2 + x_lo), y: 4, z: 16, core: 2. Of those that a mesh axis runs over, the one named last changes fastest.
Arguments:
- field: bfloat16 [192, 2, 1024, 1024], P('col', None, 'gx'), may hold values from -6 to 6
- weights: bfloat16 [64, 64, 2, 192, 192], P('gx', None, None, None, 'col'), may hold values from -4 to 4
- bias: float32 [192], P('col'), may hold values from -1 to 1
Outputs:
- activated: bfloat16 [192, 2, 1024, 1024], P('col', None, 'gx')
The draws below stay inside these ranges and needn't reach their ends.
All inputs are finite; a program needn't handle non-finite values.
Results may differ from the reference program's by a relative error of at most 0.0053.
Values may be sent and summed in bfloat16 or wider, within the bound.
A program may use at most 64 MiB of HBM per device.

```python
import math
import jax
import jax.numpy as jnp
from jax import lax

NX = 1024
NY = 1024
C = 192
MX = 64
MY = 64
PLANES = 2


def block_levels(stream_key, shape, shards, low, top_value):
    level, own = 1.0, jax.random.fold_in(stream_key, 6)
    for axis_at, parts in shards:
        heights = jnp.exp(jax.random.uniform(jax.random.fold_in(own, axis_at), (parts,), jnp.float32, low / len(shards), top_value / len(shards)))
        level = level * jnp.repeat(heights, shape[axis_at] // parts).reshape([-1 if axis == axis_at else 1 for axis in range(len(shape))])
    return level


def normal_values(own_key, extent, deviation, bound, pieces=(), dtype=jnp.bfloat16):
    factor_of = block_levels(own_key, extent, pieces, -0.22, 0.18) if pieces else 1.0
    array = jax.random.normal(own_key, extent, jnp.float32) * deviation * factor_of
    return jnp.minimum(jnp.maximum(array, -bound), bound).astype(dtype)


def setup_inputs(seed: int = 0) -> dict:
    splits = jax.random.split(jax.random.key(seed), 4)
    return {
        "field": normal_values(splits[0], (C, PLANES, NX, NY), 1.0, 6.0, ((0, 8), (2, 64))),
        "weights": normal_values(splits[1], (MY, MX, 2, C, C), 0.6, 4.0, ((0, 64), (4, 8))),
        "bias": jnp.clip(jax.random.uniform(splits[2], (C,), jnp.float32, -1.0, 1.0) * block_levels(splits[2], (C,), ((0, 8),), -0.4, 0.0), -1.0, 1.0),
    }


def second_table(count_y, count_k):
    cells = lax.iota(jnp.int32, count_y)[:, None]
    modes = lax.iota(jnp.int32, count_k)[None, :]
    phase = (modes * cells % count_y).astype(jnp.float32) * (2.0 * math.pi / count_y)
    scale = 1.0 / math.sqrt(count_y)
    return jnp.stack([jnp.cos(phase) * scale, -jnp.sin(phase) * scale], axis=-1).astype(jnp.bfloat16)

def inverse_table(count_y, count_k):
    cells = lax.iota(jnp.int32, count_y)[None, :]
    modes = lax.iota(jnp.int32, count_k)[:, None]
    phase = (modes * cells % count_y).astype(jnp.float32) * (2.0 * math.pi / count_y)
    weight = jnp.where(modes == 0, 1.0, 2.0).astype(jnp.float32) / math.sqrt(count_y)
    return jnp.stack([weight * jnp.cos(phase), -weight * jnp.sin(phase)], axis=1)

def first_tables(positions, count_x, count_k):
    modes = lax.iota(jnp.int32, count_k)
    freq = modes + jnp.where(modes >= count_k // 2, count_x - count_k, 0).astype(jnp.int32)
    phase = (positions[:, None] * freq[None, :] % count_x).astype(jnp.float32) * (2.0 * math.pi / count_x)
    scale = 1.0 / math.sqrt(count_x)
    return (jnp.cos(phase) * scale, jnp.sin(phase) * scale)

def reference(field, weights, bias):
    hp = lax.Precision.HIGHEST
    ytab = second_table(NY, MY).reshape(NY, 2 * MY)
    cosx, sinx = first_tables(lax.iota(jnp.int32, NX), NX, MX)
    gtab = inverse_table(NY, MY)

    def forward_channel(plane):
        half = jnp.dot(plane.reshape(PLANES * NX, NY), ytab, preferred_element_type=jnp.float32)
        half = jnp.transpose(half.reshape(PLANES, NX, MY, 2), (2, 3, 0, 1))
        real_part, imag_part = (half[:, 0], half[:, 1])

        def apply(m, t):
            return jnp.einsum('jpx,xk->jpk', m, t, precision=hp)
        out_real = apply(real_part, cosx) + apply(imag_part, sinx)
        out_imag = apply(imag_part, cosx) - apply(real_part, sinx)
        return jnp.stack([out_real, out_imag], axis=1)
    spectrum = lax.map(forward_channel, field)
    spectrum = jnp.transpose(spectrum, (1, 2, 0, 3, 4)).astype(jnp.bfloat16)
    spec_f = spectrum.astype(jnp.float32)
    wts_f = weights.astype(jnp.float32)

    def contract(a, b):
        return jnp.einsum('jcpk,jkco->jopk', a, b, precision=hp)
    mixed_real = contract(spec_f[:, 0], wts_f[:, :, 0]) - contract(spec_f[:, 1], wts_f[:, :, 1])
    mixed_imag = contract(spec_f[:, 0], wts_f[:, :, 1]) + contract(spec_f[:, 1], wts_f[:, :, 0])
    mixed = jnp.stack([mixed_real, mixed_imag], axis=1)

    def inverse_channel(pair):
        modes_o, bias_o = pair

        def apply(m, t):
            return jnp.einsum('jpk,xk->jpx', m, t, precision=hp)
        back_real = apply(modes_o[:, 0], cosx) - apply(modes_o[:, 1], sinx)
        back_imag = apply(modes_o[:, 1], cosx) + apply(modes_o[:, 0], sinx)
        back = jnp.stack([back_real, back_imag], axis=1)
        values = jnp.einsum('jrpx,jry->pxy', back, gtab, precision=hp)
        return jax.nn.gelu(values + bias_o, approximate=False).astype(jnp.bfloat16)
    return lax.map(inverse_channel, (jnp.moveaxis(mixed, 2, 0), bias))
```

```python
import functools
import math

import jax
import jax.numpy as jnp
import numpy as np
from jax import lax
from jax.experimental import pallas as pl
from jax.experimental.pallas import tpu as pltpu
from jax.sharding import PartitionSpec as P

MESH = pl.DeviceIdType.MESH
BF = jnp.bfloat16
F32 = jnp.float32

N = 1024
M = 64
S = 64
XL = 16
J = 8
CL = 24
PL = 2
L = CL * PL * XL


def _bf(a):
    return np.asarray(a, np.float32).astype(jnp.bfloat16)


def _split(a):
    hi = _bf(a)
    return hi, _bf(np.asarray(a, np.float64) - hi.astype(np.float64))


@functools.cache
def tables():
    y = np.arange(N)
    ky = np.arange(M)
    ang = 2 * np.pi * ((ky[:, None] * y[None, :]) % N) / N
    sc = 1 / math.sqrt(N)
    yt = _bf(np.stack([np.cos(ang) * sc, -np.sin(ang) * sc], 1).reshape(2 * M, N))
    wgt = np.where(ky == 0, 1.0, 2.0)[:, None]
    g = np.stack([wgt * np.cos(ang) * sc, -wgt * np.sin(ang) * sc], 1).reshape(2 * M, N)
    g2 = np.concatenate(_split(g), 0)

    k = np.arange(M)
    s = np.arange(S)
    ph = 2 * np.pi * ((k[:, None] * s[None, :]) % S) / S
    c, d = np.cos(ph) * sc, np.sin(ph) * sc
    dm = np.zeros((2, M, S, 2))
    dm[0, :, :, 0], dm[0, :, :, 1] = c, d
    dm[1, :, :, 0], dm[1, :, :, 1] = -d, c
    d2 = np.concatenate(_split(dm.reshape(2 * M, 2 * S)), 1)

    f = np.where(k < M // 2, k, k - M)
    tw = 2 * np.pi * f[:, None] * np.arange(XL)[None, :] / N
    tct = np.tile(np.cos(tw), (1, 8))
    tst = np.tile(np.sin(tw), (1, 8))

    bm = np.zeros((2, CL, PL, XL, 2, PL, 32), np.float32)
    for ci in range(CL):
        for p in range(PL):
            for r in range(2):
                bm[r, ci, p, :, r, p, ci] = 1
    bm = _bf(bm.reshape(2 * L, 128))

    pm = np.zeros((J, 4, 32, 256), np.float32)
    for j in range(J):
        for ci in range(CL):
            pm[j, :, ci, j * CL + ci] = 1
    pm = _bf(pm.reshape(J * 128, 256))
    qm = np.zeros((4, J, 4, 32), np.float32)
    for q in range(4):
        qm[q, :, q] = 1
    qm = _bf(np.broadcast_to(qm.reshape(4, 1, J * 128), (4, 16, J * 128)).reshape(64, J * 128))

    mask = np.zeros((8, 8, 2, CL), np.float32)
    for i in range(8):
        mask[i, i] = 1
    mask = mask.reshape(8, 384)
    fe = np.zeros((8, 2, CL, 2, CL, XL), np.float32)
    for w in range(2):
        for o in range(CL):
            fe[:, w, o, w, o, :] = 1
    fe = _bf(fe.reshape(384, L))

    t2 = lambda t: np.broadcast_to(
        t.reshape(8, 1, 8, 128), (8, 2, 8, 128)).reshape(128, 128)
    e = np.zeros((S, 2, 2, 8, 2, 8))
    for ab in range(2):
        for r in range(2):
            val = np.exp(1j * ph.T) * (1j ** (r + ab)) * sc
            e[:, 0, ab, :, r] = val.real.reshape(S, 8, 8)
            e[:, 1, ab, :, r] = val.imag.reshape(S, 8, 8)
    ehi, elo = _split(e.reshape(2 * S, 256))
    ee = np.concatenate([ehi, elo], 0)
    tf = np.concatenate([tct, tst, t2(tct), t2(tst)], 0).astype(np.float32)
    return dict(yt=yt, g2=g2, d2=d2, tf=tf, bm=bm, pm=pm, qm=qm, mask=mask, fe=fe, ee=ee)


def split(v):
    hi = v.astype(BF)
    return hi, (v - hi.astype(F32)).astype(BF)


def dot(a, b):
    return jnp.dot(a, b, preferred_element_type=F32)


def dot_nt(a, b):
    return lax.dot_general(a, b, (((1,), (1,)), ((), ())), preferred_element_type=F32)


NAMES = ("yt", "d2", "tf", "bm", "pm", "qm", "mask", "fe", "ee")


def exchange_kernel(*refs):
    nt = len(NAMES)
    field_h, w_h = refs[:2]
    tabs_h = refs[2:2 + nt]
    back_ref = refs[2 + nt]
    fbuf, wbuf = refs[3 + nt:5 + nt]
    tabs = dict(zip(NAMES, refs[5 + nt:5 + 2 * nt]))
    (send1, recv1, ags, agr, send2, recv2,
     in_sem, loc_sem, s1, r1, sa, ra, s2, r2) = refs[5 + 2 * nt:]

    me = lax.axis_index("gx")
    mc = lax.axis_index("col")

    barrier = pltpu.get_barrier_semaphore()

    def greet_gx(i, _):
        pl.semaphore_signal(barrier, inc=1, device_id={"gx": lax.rem(me + i, S)}, device_id_type=MESH)
        return 0

    def greet_col(i, _):
        pl.semaphore_signal(barrier, inc=1, device_id={"col": lax.rem(mc + i, J)}, device_id_type=MESH)
        return 0

    lax.fori_loop(1, S, greet_gx, 0)
    lax.fori_loop(1, J, greet_col, 0)

    copies = [pltpu.make_async_copy(field_h, fbuf, in_sem.at[0])]
    copies += [pltpu.make_async_copy(h, tabs[n], in_sem.at[2 + i])
               for i, (h, n) in enumerate(zip(tabs_h, NAMES))]
    copies += [pltpu.make_async_copy(w_h, wbuf, in_sem.at[1])]
    for c in copies:
        c.start()
    copies[0].wait()
    copies[1].wait()

    h = dot_nt(tabs["yt"][...], fbuf[...])
    send1[...] = h.astype(BF).reshape(S, 2, L)

    pl.semaphore_wait(barrier, S - 1 + J - 1)

    def offset(i):
        half = lax.div(i + 1, 2)
        return jnp.where(lax.rem(i, 2) == 1, S // 2 - half, S // 2 + half)

    def exchange(send, recv, ssem, rsem):
        own = pltpu.make_async_copy(send.at[me], recv.at[me], loc_sem)
        own.start()

        def go(i, _):
            t = lax.rem(me + offset(i), S)
            pltpu.make_async_remote_copy(
                src_ref=send.at[t], dst_ref=recv.at[me], send_sem=ssem.at[t], recv_sem=rsem.at[me],
                device_id={"gx": t}, device_id_type=MESH).start()
            return 0

        lax.fori_loop(0, S - 1, go, 0)
        own.wait()

    def arrive(send, recv, ssem, rsem):
        def one(i, _):
            t = lax.rem(me + i, S)
            pltpu.make_async_remote_copy(
                src_ref=send.at[t], dst_ref=recv.at[t], send_sem=ssem.at[t], recv_sem=rsem.at[t],
                device_id={"gx": t}, device_id_type=MESH).wait_recv()
            return 0

        lax.fori_loop(1, S, one, 0)

    def drain(send, recv, ssem, rsem):
        def one(i, _):
            t = lax.rem(me + i, S)
            pltpu.make_async_remote_copy(
                src_ref=send.at[t], dst_ref=recv.at[t], send_sem=ssem.at[t], recv_sem=rsem.at[t],
                device_id={"gx": t}, device_id_type=MESH).wait_send()
            return 0

        lax.fori_loop(1, S, one, 0)

    exchange(send1, recv1, s1, r1)
    for c in copies[2:]:
        c.wait()
    arrive(send1, recv1, s1, r1)

    got = recv1[...].reshape(2 * S, L)
    g = dot(tabs["d2"][...], jnp.concatenate([got, got], 0))
    tc = jnp.concatenate([tabs["tf"][0:64]] * 6, 1)
    ts = jnp.concatenate([tabs["tf"][64:128]] * 6, 1)
    gr, gi = g[:M], g[M:]
    prh, prl = split(tc * gr + ts * gi)
    pih, pil = split(tc * gi - ts * gr)
    bm = tabs["bm"]
    sp = dot(jnp.concatenate([prh, pih], 1), bm[...]) + dot(jnp.concatenate([prl, pil], 1), bm[...])
    ags[...] = sp.astype(BF)

    own = pltpu.make_async_copy(ags, agr.at[mc], loc_sem)
    own.start()

    def col_copy(i):
        t = lax.rem(mc + i, J)
        return t, lambda slot: pltpu.make_async_remote_copy(
            src_ref=ags, dst_ref=agr.at[slot], send_sem=sa.at[t], recv_sem=ra.at[slot],
            device_id={"col": t}, device_id_type=MESH)

    def col_go(i, _):
        t, make = col_copy(i)
        make(mc).start()
        return 0

    def col_in(i, _):
        t, make = col_copy(i)
        make(t).wait_recv()
        return 0

    def col_out(i, _):
        t, make = col_copy(i)
        make(t).wait_send()
        return 0

    lax.fori_loop(1, J, col_go, 0)
    own.wait()
    drain(send1, recv1, s1, r1)
    lax.fori_loop(1, J, col_in, 0)

    a = jnp.concatenate([agr[j] for j in range(J)], 1)
    qm = tabs["qm"]
    lhs = []
    for q in range(4):
        m = jnp.concatenate([qm[16 * q:16 * q + 16]] * 4, 0)
        lhs.append(a * m)
    full = dot(jnp.concatenate(lhs, 0), tabs["pm"][...])
    mask = tabs["mask"][...]
    zh, zl = [], []
    for kg in range(8):
        rows = jnp.concatenate([full[64 * q + 8 * kg:64 * q + 8 * kg + 8, :192] for q in range(4)], 0)
        z = dot_nt(rows.astype(BF), wbuf[384 * kg:384 * kg + 384, :])
        hi, lo = split(z * jnp.concatenate([mask] * 4, 0))
        zh.append(hi)
        zl.append(lo)
    fe = tabs["fe"][...]
    yv = dot(jnp.concatenate(zh, 0), fe) + dot(jnp.concatenate(zl, 0), fe)
    tc2 = jnp.concatenate([tabs["tf"][128:256]] * 3, 1)
    ts2 = jnp.concatenate([tabs["tf"][256:384]] * 3, 1)
    aa, bb = [], []
    for p in range(PL):
        yp = jnp.concatenate(
            [yv[32 * kg + 16 * r + 8 * p:32 * kg + 16 * r + 8 * p + 8] for kg in range(8) for r in range(2)], 0)
        y0, y1 = yp[:, :384], yp[:, 384:]
        aa.append(tc2 * y0 - ts2 * y1)
        bb.append(tc2 * y1 + ts2 * y0)
    ab = jnp.concatenate([jnp.concatenate(aa, 1), jnp.concatenate(bb, 1)], 0)
    abh, abl = split(ab)
    ee = tabs["ee"]
    wide = dot(ee[:128], abh) + dot(ee[128:], abh) + dot(ee[:128], abl)
    send2[...] = wide.astype(BF).reshape(S, 2, L)

    exchange(send2, recv2, s2, r2)
    lax.fori_loop(1, J, col_out, 0)
    arrive(send2, recv2, s2, r2)
    back_ref[...] = recv2[...].reshape(2 * S, L)
    drain(send2, recv2, s2, r2)


def exchanges(field, w, tabs):
    ops = [tabs[n] for n in NAMES]
    vm = [pltpu.VMEM((L, N), BF), pltpu.VMEM((M * 2 * CL, J * CL), BF)]
    vm += [pltpu.VMEM(t.shape, t.dtype) for t in ops]
    msg = pltpu.VMEM((S, 2, L), BF)
    dma = pltpu.SemaphoreType.DMA
    return pl.pallas_call(
        exchange_kernel,
        out_shape=jax.ShapeDtypeStruct((2 * S, L), BF),
        in_specs=[pl.BlockSpec(memory_space=pl.ANY)] * (2 + len(ops)),
        out_specs=pl.BlockSpec(memory_space=pltpu.VMEM),
        scratch_shapes=vm + [
            msg, msg, pltpu.VMEM((M, 128), BF), pltpu.VMEM((J, M, 128), BF), msg, msg,
            dma((2 + len(ops),)), dma,
            dma((S,)), dma((S,)), dma((J,)), dma((J,)), dma((S,)), dma((S,))],
        compiler_params=pltpu.CompilerParams(
            collective_id=0, has_side_effects=True, vmem_limit_bytes=40 * 2**20),
        name="exchange",
    )(field, w, *ops)


def finish_kernel(back_ref, g_ref, bias_ref, out_ref):
    b = back_ref[...]
    v = lax.dot_general(jnp.concatenate([b, b], 0), g_ref[...], (((0,), (0,)), ((), ())),
                        preferred_element_type=F32)
    v = v + bias_ref[...]
    u = 0.5 * v * (1.0 + lax.erf(v * math.sqrt(0.5)))
    out_ref[...] = u.astype(BF).reshape(out_ref.shape)


def finish(back, g2, bias_rows):
    ob = 8
    rows = ob * XL
    return pl.pallas_call(
        finish_kernel,
        out_shape=jax.ShapeDtypeStruct((CL, PL, XL, N), BF),
        grid=(PL, CL // ob),
        in_specs=[
            pl.BlockSpec((2 * S, rows), lambda p, i: (0, p * (CL // ob) + i)),
            pl.BlockSpec((4 * M, N), lambda p, i: (0, 0)),
            pl.BlockSpec((rows, 1), lambda p, i: (i, 0)),
        ],
        out_specs=pl.BlockSpec((ob, None, XL, N), lambda p, i: (i, p, 0, 0)),
        name="finish",
    )(back, g2, bias_rows)


def body(field, weights, bias):
    tabs = {n: jnp.asarray(t) for n, t in tables().items()}
    w = jnp.swapaxes(weights, 3, 4).reshape(M * 2 * CL, J * CL)
    back = exchanges(field.reshape(L, N), w, tabs)
    return finish(back, tabs["g2"], jnp.repeat(bias, XL)[:, None])


def solution(mesh):
    placed = (P("col", None, "gx", None), P("gx", None, None, None, "col"), P("col"))
    return jax.shard_map(
        body, mesh=mesh, in_specs=placed, out_specs=P("col", None, "gx", None), check_vma=False
    )
```

```python
import functools
import math

import jax
import jax.numpy as jnp
import numpy as np
from jax import lax
from jax.experimental import pallas as pl
from jax.experimental.pallas import tpu as pltpu
from jax.sharding import PartitionSpec as P

MESH = pl.DeviceIdType.MESH
BF = jnp.bfloat16
F32 = jnp.float32

N = 1024
M = 64
S = 64
XL = 16
J = 8
CL = 24
PL = 2
H = CL * XL


def _bf(a):
    return np.asarray(a, np.float32).astype(jnp.bfloat16)


def _split(a):
    hi = _bf(a)
    return hi, _bf(np.asarray(a, np.float64) - hi.astype(np.float64))


@functools.cache
def tables():
    y = np.arange(N)
    ky = np.arange(M)
    ang = 2 * np.pi * ((ky[:, None] * y[None, :]) % N) / N
    sc = 1 / math.sqrt(N)
    yt = _bf(np.stack([np.cos(ang) * sc, -np.sin(ang) * sc], 1).reshape(2 * M, N))
    wgt = np.where(ky == 0, 1.0, 2.0)[:, None]
    g = np.stack([wgt * np.cos(ang) * sc, -wgt * np.sin(ang) * sc], 1).reshape(2 * M, N)
    g2 = np.concatenate(_split(g), 0)

    k = np.arange(M)
    s = np.arange(S)
    ph = 2 * np.pi * ((k[:, None] * s[None, :]) % S) / S
    c, d = np.cos(ph) * sc, np.sin(ph) * sc
    dm = np.zeros((2, M, S, 2))
    dm[0, :, :, 0], dm[0, :, :, 1] = c, d
    dm[1, :, :, 0], dm[1, :, :, 1] = -d, c
    d2 = np.concatenate(_split(dm.reshape(2 * M, 2 * S)), 1)

    f = np.where(k < M // 2, k, k - M)
    tw = 2 * np.pi * f[:, None] * np.arange(XL)[None, :] / N
    tct = np.tile(np.cos(tw), (1, 8))
    tst = np.tile(np.sin(tw), (1, 8))

    bt = np.zeros((CL, CL, XL), np.float32)
    ex = np.zeros((2, 2, CL, 2, CL, XL), np.float32)
    for o in range(CL):
        bt[o, o] = 1
        for w in range(2):
            ex[:, w, o, w, o, :] = 1
    bt = _bf(bt.reshape(CL, H))
    ex = _bf(ex.reshape(4 * CL, 2 * H))

    e = np.zeros((S, 2, 2, 2, M))
    for ab in range(2):
        for r in range(2):
            val = np.exp(1j * ph.T) * (1j ** (r + ab)) * sc
            e[:, 0, ab, r] = val.real
            e[:, 1, ab, r] = val.imag
    ehi, elo = _split(e.reshape(2 * S, 256))
    ee = np.concatenate([ehi, elo], 0)
    tf = np.concatenate([tct, tst], 0).astype(np.float32)
    return dict(yt=yt, g2=g2, d2=d2, tf=tf, bt=bt, ex=ex, ee=ee)


def split(v):
    hi = v.astype(BF)
    return hi, (v - hi.astype(F32)).astype(BF)


def dot(a, b):
    return jnp.dot(a, b, preferred_element_type=F32)


def dot_nt(a, b):
    return lax.dot_general(a, b, (((1,), (1,)), ((), ())), preferred_element_type=F32)


NAMES = ("yt", "d2", "tf", "bt", "ex", "ee", "g2")


def exchange_kernel(*refs):
    nt = len(NAMES)
    field_h, w_h, bias_h = refs[:3]
    tabs_h = refs[3:3 + nt]
    out_h = refs[3 + nt]
    fbuf, wbuf, bias_s = refs[4 + nt:7 + nt]
    tabs = dict(zip(NAMES, refs[7 + nt:7 + 2 * nt]))
    (send1, recv1, ags, agr, send2, recv2, obuf,
     in_sem, loc_sem, s1, r1, sa, ra, s2, r2, out_sem) = refs[7 + 2 * nt:]

    me = lax.axis_index("gx")
    mc = lax.axis_index("col")

    first = [pltpu.make_async_copy(tabs_h[0], tabs["yt"], in_sem.at[0])]
    first += [pltpu.make_async_copy(field_h.at[:, p], fbuf.at[p], in_sem.at[1 + p]) for p in range(PL)]
    rest = [pltpu.make_async_copy(h, tabs[n], in_sem.at[5 + i])
            for i, (h, n) in enumerate(zip(tabs_h[1:], NAMES[1:]))]
    rest += [pltpu.make_async_copy(w_h, wbuf, in_sem.at[3]),
             pltpu.make_async_copy(bias_h, bias_s, in_sem.at[4])]
    for c in first:
        c.start()

    barrier = pltpu.get_barrier_semaphore()

    def hello(axis, t):
        pl.semaphore_signal(barrier, inc=1, device_id={axis: t}, device_id_type=MESH)

    def around(go):
        go(lax.rem(me + S // 2, S))

        def pair(i, _):
            go(lax.rem(me + S // 2 - i, S))
            go(lax.rem(me + S // 2 + i, S))
            return 0

        lax.fori_loop(1, S // 2, pair, 0)

    def greet_col(i, _):
        hello("col", lax.rem(mc + i, J))
        return 0

    around(lambda t: hello("gx", t))
    lax.fori_loop(1, J, greet_col, 0)
    for c in rest:
        c.start()
    first[0].wait()
    for p in range(PL):
        first[1 + p].wait()
        h = dot_nt(tabs["yt"][...], fbuf[p].reshape(H, N))
        send1[p] = h.astype(BF).reshape(S, 2, H)

    pl.semaphore_wait(barrier, S - 1 + J - 1)

    def message(t, slot, send, recv, ssem, rsem):
        return pltpu.make_async_remote_copy(
            src_ref=send.at[t], dst_ref=recv.at[slot], send_sem=ssem.at[t], recv_sem=rsem.at[slot],
            device_id={"gx": t}, device_id_type=MESH)

    def exchange(*refs):
        own = pltpu.make_async_copy(refs[0].at[me], refs[1].at[me], loc_sem)
        own.start()
        around(lambda t: message(t, me, *refs).start())
        own.wait()

    def others(wait):
        def one(i, _):
            wait(lax.rem(me + i, S))
            return 0

        lax.fori_loop(1, S, one, 0)

    def arrive(*refs):
        others(lambda t: message(t, t, *refs).wait_recv())

    def drain(*refs):
        others(lambda t: message(t, t, *refs).wait_send())

    def port(send, recv, ssem, rsem, p):
        return send.at[p], recv.at[p], ssem.at[p], rsem.at[p]

    ports1 = [port(send1, recv1, s1, r1, p) for p in range(PL)]
    ports2 = [port(send2, recv2, s2, r2, p) for p in range(PL)]

    def columns(wait, p):
        def one(i, _):
            t = lax.rem(mc + i, J)
            slot = mc if wait is None else t
            c = pltpu.make_async_remote_copy(
                src_ref=ags.at[p], dst_ref=agr.at[p, slot], send_sem=sa.at[p, t], recv_sem=ra.at[p, slot],
                device_id={"col": t}, device_id_type=MESH)
            if wait is None:
                c.start()
            elif wait:
                c.wait_recv()
            else:
                c.wait_send()
            return 0

        lax.fori_loop(1, J, one, 0)

    for p in range(PL):
        exchange(*ports1[p])
    for c in rest:
        c.wait()

    tc = jnp.concatenate([tabs["tf"][0:M]] * 3, 1)
    ts = jnp.concatenate([tabs["tf"][M:2 * M]] * 3, 1)
    for p in range(PL):
        arrive(*ports1[p])
        got = recv1[p].reshape(2 * S, H)
        g = dot(tabs["d2"][...], jnp.concatenate([got, got], 0))
        gr, gi = g[:M], g[M:]
        hi, lo = split(jnp.concatenate([tc * gr + ts * gi, tc * gi - ts * gr], 0))
        bt = tabs["bt"][...]
        ags[p] = (dot_nt(bt, hi) + dot_nt(bt, lo)).astype(BF)
        own = pltpu.make_async_copy(ags.at[p], agr.at[p, mc], loc_sem)
        own.start()
        columns(None, p)
        own.wait()

    lane = lax.broadcasted_iota(jnp.int32, (2 * CL, 2 * M), 1) % M
    tc = jnp.concatenate([tc, tc], 0)
    ts = jnp.concatenate([ts, ts], 0)
    for p in range(PL):
        columns(True, p)
        a = agr[p].reshape(J * CL, 2 * M)
        mixed = jnp.zeros((2 * CL, 2 * M), F32)
        for kg in range(8):
            z = dot(wbuf[384 * kg:384 * kg + 384, :], a)
            for i in range(8):
                mixed = jnp.where(lane == 8 * kg + i, z[48 * i:48 * i + 48], mixed)
        hi, lo = split(mixed)
        y = lax.dot_general(jnp.concatenate([hi, lo], 0), tabs["ex"][...], (((0,), (0,)), ((), ())),
                            preferred_element_type=F32)
        y0, y1 = y[:, :H], y[:, H:]
        hi, lo = split(jnp.concatenate([tc * y0 - ts * y1, tc * y1 + ts * y0], 0))
        ee = tabs["ee"]
        wide = dot(ee[:128], hi) + dot(ee[128:], hi) + dot(ee[:128], lo)
        send2[p] = wide.astype(BF).reshape(S, 2, H)
        exchange(*ports2[p])

    for p in range(PL):
        drain(*ports1[p])
        columns(False, p)
    g2 = tabs["g2"]
    ob = 8
    puts = []
    for p in range(PL):
        arrive(*ports2[p])
        got = recv2[p].reshape(2 * S, H)
        got = jnp.concatenate([got, got], 0)
        for n in range(CL // ob):
            v = lax.dot_general(got[:, 128 * n:128 * n + 128], g2[...], (((0,), (0,)), ((), ())),
                                preferred_element_type=F32)
            for i in range(ob):
                o = n * ob + i
                u = v[XL * i:XL * i + XL] + bias_s[o]
                u = 0.5 * u * (1.0 + lax.erf(u * math.sqrt(0.5)))
                obuf[p, o] = u.astype(BF)
            put = pltpu.make_async_copy(
                obuf.at[p, pl.ds(n * ob, ob)], out_h.at[pl.ds(n * ob, ob), p], out_sem.at[p, n])
            put.start()
            puts.append(put)
    for p in range(PL):
        drain(*ports2[p])
    for put in puts:
        put.wait()


def exchanges(field, w, bias, tabs):
    ops = [tabs[n] for n in NAMES]
    vm = [pltpu.VMEM((PL, CL, XL, N), BF), pltpu.VMEM((M * 2 * CL, J * CL), BF), pltpu.SMEM((CL,), F32)]
    vm += [pltpu.VMEM(t.shape, t.dtype) for t in ops]
    msg = pltpu.VMEM((PL, S, 2, H), BF)
    dma = pltpu.SemaphoreType.DMA
    return pl.pallas_call(
        exchange_kernel,
        out_shape=jax.ShapeDtypeStruct((CL, PL, XL, N), BF),
        in_specs=[pl.BlockSpec(memory_space=pl.ANY)] * (3 + len(ops)),
        out_specs=pl.BlockSpec(memory_space=pl.ANY),
        scratch_shapes=vm + [
            msg, msg, pltpu.VMEM((PL, CL, 2 * M), BF), pltpu.VMEM((PL, J, CL, 2 * M), BF), msg, msg,
            pltpu.VMEM((PL, CL, XL, N), BF),
            dma((4 + len(ops),)), dma,
            dma((PL, S)), dma((PL, S)), dma((PL, J)), dma((PL, J)), dma((PL, S)), dma((PL, S)), dma((PL, 3))],
        compiler_params=pltpu.CompilerParams(
            collective_id=0, has_side_effects=True, vmem_limit_bytes=67043328),
        name="exchange",
    )(field, w, bias, *ops)


def body(field, weights, bias):
    tabs = {n: jnp.asarray(t) for n, t in tables().items()}
    w = jnp.swapaxes(weights, 3, 4).reshape(M * 2 * CL, J * CL)
    return exchanges(field, w, bias, tabs)


def solution(mesh):
    placed = (P("col", None, "gx", None), P("gx", None, None, None, "col"), P("col"))
    return jax.shard_map(
        body, mesh=mesh, in_specs=placed, out_specs=P("col", None, "gx", None), check_vma=False
    )
```

```python
import functools
import math

import jax
import jax.numpy as jnp
import numpy as np
from jax import lax
from jax.experimental import pallas as pl
from jax.experimental.pallas import tpu as pltpu
from jax.sharding import PartitionSpec as P

MESH = pl.DeviceIdType.MESH
BF = jnp.bfloat16
F32 = jnp.float32

N = 1024
M = 64
S = 64
XL = 16
J = 8
CL = 24
PL = 2
H = CL * XL


def _bf(a):
    return np.asarray(a, np.float32).astype(jnp.bfloat16)


def _split(a):
    hi = _bf(a)
    return hi, _bf(np.asarray(a, np.float64) - hi.astype(np.float64))


@functools.cache
def tables():
    y = np.arange(N)
    ky = np.arange(M)
    ang = 2 * np.pi * ((ky[:, None] * y[None, :]) % N) / N
    sc = 1 / math.sqrt(N)
    yt = _bf(np.stack([np.cos(ang) * sc, -np.sin(ang) * sc], 1).reshape(2 * M, N))
    wgt = np.where(ky == 0, 1.0, 2.0)[:, None]
    g = np.stack([wgt * np.cos(ang) * sc, -wgt * np.sin(ang) * sc], 1).reshape(2 * M, N)
    g2 = np.concatenate(_split(g), 0)

    k = np.arange(M)
    s = np.arange(S)
    ph = 2 * np.pi * ((k[:, None] * s[None, :]) % S) / S
    c, d = np.cos(ph) * sc, np.sin(ph) * sc
    dm = np.zeros((2, M, S, 2))
    dm[0, :, :, 0], dm[0, :, :, 1] = c, d
    dm[1, :, :, 0], dm[1, :, :, 1] = -d, c
    d2 = np.concatenate(_split(dm.reshape(2 * M, 2 * S)), 1)

    f = np.where(k < M // 2, k, k - M)
    tw = 2 * np.pi * f[:, None] * np.arange(XL)[None, :] / N
    tct = np.tile(np.cos(tw), (1, 8))
    tst = np.tile(np.sin(tw), (1, 8))

    bt = np.zeros((CL, CL, XL), np.float32)
    ex = np.zeros((2, 2, CL, 2, CL, XL), np.float32)
    for o in range(CL):
        bt[o, o] = 1
        for w in range(2):
            ex[:, w, o, w, o, :] = 1
    bt = _bf(bt.reshape(CL, H))
    ex = _bf(ex.reshape(4 * CL, 2 * H))

    e = np.zeros((S, 2, 2, 2, M))
    for ab in range(2):
        for r in range(2):
            val = np.exp(1j * ph.T) * (1j ** (r + ab)) * sc
            e[:, 0, ab, r] = val.real
            e[:, 1, ab, r] = val.imag
    ehi, elo = _split(e.reshape(2 * S, 256))
    ee = np.concatenate([ehi, elo], 0)
    tf = np.concatenate([tct, tst], 0).astype(np.float32)
    return dict(yt=yt, g2=g2, d2=d2, tf=tf, bt=bt, ex=ex, ee=ee)


def split(v):
    hi = v.astype(BF)
    return hi, (v - hi.astype(F32)).astype(BF)


def dot(a, b):
    return jnp.dot(a, b, preferred_element_type=F32)


def dot_nt(a, b):
    return lax.dot_general(a, b, (((1,), (1,)), ((), ())), preferred_element_type=F32)


NAMES = ("yt", "d2", "tf", "bt", "ex", "ee", "g2")


def exchange_kernel(*refs):
    nt = len(NAMES)
    field_h, w_h, bias_h = refs[:3]
    tabs_h = refs[3:3 + nt]
    out_h = refs[3 + nt]
    fbuf, wbuf, bias_s = refs[4 + nt:7 + nt]
    tabs = dict(zip(NAMES, refs[7 + nt:7 + 2 * nt]))
    (send1, recv1, ags, agr, send2, recv2, obuf,
     in_sem, loc_sem, s1, r1, sa, ra, s2, r2, out_sem) = refs[7 + 2 * nt:]

    me = lax.axis_index("gx")
    mc = lax.axis_index("col")

    first = [pltpu.make_async_copy(tabs_h[0], tabs["yt"], in_sem.at[0])]
    first += [pltpu.make_async_copy(field_h.at[:, p], fbuf.at[p], in_sem.at[1 + p]) for p in range(PL)]
    rest = [pltpu.make_async_copy(h, tabs[n], in_sem.at[5 + i])
            for i, (h, n) in enumerate(zip(tabs_h[1:], NAMES[1:]))]
    rest += [pltpu.make_async_copy(w_h, wbuf, in_sem.at[3]),
             pltpu.make_async_copy(bias_h, bias_s, in_sem.at[4])]
    for c in first:
        c.start()

    barrier = pltpu.get_barrier_semaphore()

    def hello(axis, t):
        pl.semaphore_signal(barrier, inc=1, device_id={axis: t}, device_id_type=MESH)

    def around(go):
        go(lax.rem(me + S // 2, S))

        def step(i, _):
            for n in range(3):
                d = 3 * i + n + 1
                go(lax.rem(me + S // 2 - d, S))
                go(lax.rem(me + S // 2 + d, S))
            return 0

        lax.fori_loop(0, 10, step, 0)
        go(lax.rem(me + 1, S))
        go(lax.rem(me + S - 1, S))

    def greet_col(i, _):
        hello("col", lax.rem(mc + i, J))
        return 0

    around(lambda t: hello("gx", t))
    lax.fori_loop(1, J, greet_col, 0)
    for c in rest:
        c.start()
    first[0].wait()
    for p in range(PL):
        first[1 + p].wait()
        h = dot_nt(tabs["yt"][...], fbuf[p].reshape(H, N))
        send1[p] = h.astype(BF).reshape(S, 2, H)

    pl.semaphore_wait(barrier, S - 1 + J - 1)

    def message(t, send, recv, ssem, rsem):
        return pltpu.make_async_remote_copy(
            src_ref=send.at[t], dst_ref=recv.at[me], send_sem=ssem, recv_sem=rsem,
            device_id={"gx": t}, device_id_type=MESH)

    def exchange(*refs):
        own = pltpu.make_async_copy(refs[0].at[me], refs[1].at[me], loc_sem)
        own.start()
        around(lambda t: message(t, *refs).start())
        own.wait()

    def others(send, recv, ssem, rsem):
        every = pl.ds(0, S - 1)
        return pltpu.make_async_remote_copy(
            src_ref=send.at[every], dst_ref=recv.at[every], send_sem=ssem, recv_sem=rsem,
            device_id={"gx": lax.rem(me + 1, S)}, device_id_type=MESH)

    def arrive(*refs):
        others(*refs).wait_recv()

    def drain(*refs):
        others(*refs).wait_send()

    def port(send, recv, ssem, rsem, p):
        return send.at[p], recv.at[p], ssem.at[p], rsem.at[p]

    ports1 = [port(send1, recv1, s1, r1, p) for p in range(PL)]
    ports2 = [port(send2, recv2, s2, r2, p) for p in range(PL)]

    def columns(p):
        own = pltpu.make_async_copy(ags.at[p], agr.at[p, mc], loc_sem)
        own.start()

        def one(i, _):
            pltpu.make_async_remote_copy(
                src_ref=ags.at[p], dst_ref=agr.at[p, mc], send_sem=sa.at[p], recv_sem=ra.at[p],
                device_id={"col": lax.rem(mc + i, J)}, device_id_type=MESH).start()
            return 0

        lax.fori_loop(1, J, one, 0)
        own.wait()

    def column_bytes(p):
        every = agr.at[p, pl.ds(0, J - 1)]
        return pltpu.make_async_remote_copy(
            src_ref=every, dst_ref=every, send_sem=sa.at[p], recv_sem=ra.at[p],
            device_id={"col": lax.rem(mc + 1, J)}, device_id_type=MESH)

    for p in range(PL):
        exchange(*ports1[p])
    for c in rest:
        c.wait()

    tc = jnp.concatenate([tabs["tf"][0:M]] * 3, 1)
    ts = jnp.concatenate([tabs["tf"][M:2 * M]] * 3, 1)
    for p in range(PL):
        arrive(*ports1[p])
        got = recv1[p].reshape(2 * S, H)
        g = dot(tabs["d2"][...], jnp.concatenate([got, got], 0))
        gr, gi = g[:M], g[M:]
        hi, lo = split(jnp.concatenate([tc * gr + ts * gi, tc * gi - ts * gr], 0))
        bt = tabs["bt"][...]
        ags[p] = (dot_nt(bt, hi) + dot_nt(bt, lo)).astype(BF)
        columns(p)

    lane = lax.broadcasted_iota(jnp.int32, (2 * CL, 2 * M), 1) % M
    tc = jnp.concatenate([tc, tc], 0)
    ts = jnp.concatenate([ts, ts], 0)
    for p in range(PL):
        column_bytes(p).wait_recv()
        a = agr[p].reshape(J * CL, 2 * M)
        mixed = jnp.zeros((2 * CL, 2 * M), F32)
        for kg in range(8):
            z = dot(wbuf[384 * kg:384 * kg + 384, :], a)
            for i in range(8):
                mixed = jnp.where(lane == 8 * kg + i, z[48 * i:48 * i + 48], mixed)
        hi, lo = split(mixed)
        y = lax.dot_general(jnp.concatenate([hi, lo], 0), tabs["ex"][...], (((0,), (0,)), ((), ())),
                            preferred_element_type=F32)
        y0, y1 = y[:, :H], y[:, H:]
        hi, lo = split(jnp.concatenate([tc * y0 - ts * y1, tc * y1 + ts * y0], 0))
        ee = tabs["ee"]
        wide = dot(ee[:128], hi) + dot(ee[128:], hi) + dot(ee[:128], lo)
        send2[p] = wide.astype(BF).reshape(S, 2, H)
        exchange(*ports2[p])

    for p in range(PL):
        drain(*ports1[p])
        column_bytes(p).wait_send()
    g2 = tabs["g2"]
    ob = 8
    puts = []
    for p in range(PL):
        arrive(*ports2[p])
        got = recv2[p].reshape(2 * S, H)
        got = jnp.concatenate([got, got], 0)
        for n in range(CL // ob):
            v = lax.dot_general(got[:, 128 * n:128 * n + 128], g2[...], (((0,), (0,)), ((), ())),
                                preferred_element_type=F32)
            for i in range(ob):
                o = n * ob + i
                u = v[XL * i:XL * i + XL] + bias_s[o]
                u = 0.5 * u * (1.0 + lax.erf(u * math.sqrt(0.5)))
                obuf[p, o] = u.astype(BF)
            put = pltpu.make_async_copy(
                obuf.at[p, pl.ds(n * ob, ob)], out_h.at[pl.ds(n * ob, ob), p], out_sem.at[p, n])
            put.start()
            puts.append(put)
    for p in range(PL):
        drain(*ports2[p])
    for put in puts:
        put.wait()


def exchanges(field, w, bias, tabs):
    ops = [tabs[n] for n in NAMES]
    vm = [pltpu.VMEM((PL, CL, XL, N), BF), pltpu.VMEM((M * 2 * CL, J * CL), BF), pltpu.SMEM((CL,), F32)]
    vm += [pltpu.VMEM(t.shape, t.dtype) for t in ops]
    msg = pltpu.VMEM((PL, S, 2, H), BF)
    dma = pltpu.SemaphoreType.DMA
    return pl.pallas_call(
        exchange_kernel,
        out_shape=jax.ShapeDtypeStruct((CL, PL, XL, N), BF),
        in_specs=[pl.BlockSpec(memory_space=pl.ANY)] * (3 + len(ops)),
        out_specs=pl.BlockSpec(memory_space=pl.ANY),
        scratch_shapes=vm + [
            msg, msg, pltpu.VMEM((PL, CL, 2 * M), BF), pltpu.VMEM((PL, J, CL, 2 * M), BF), msg, msg,
            pltpu.VMEM((PL, CL, XL, N), BF),
            dma((4 + len(ops),)), dma,
            dma((PL,)), dma((PL,)), dma((PL,)), dma((PL,)), dma((PL,)), dma((PL,)), dma((PL, 3))],
        compiler_params=pltpu.CompilerParams(
            collective_id=0, has_side_effects=True, vmem_limit_bytes=24 * 2**20),
        name="exchange",
    )(*[pltpu.with_memory_space_constraint(v, pltpu.HBM) for v in (field, w, bias, *ops)])


def body(field, weights, bias):
    tabs = {n: jnp.asarray(t) for n, t in tables().items()}
    w = jnp.swapaxes(weights, 3, 4).reshape(M * 2 * CL, J * CL)
    return exchanges(field, w, bias, tabs)


def solution(mesh):
    placed = (P("col", None, "gx", None), P("gx", None, None, None, "col"), P("col"))
    return jax.shard_map(
        body, mesh=mesh, in_specs=placed, out_specs=P("col", None, "gx", None), check_vma=False
    )
```

```python
import functools
import math

import jax
import jax.numpy as jnp
import numpy as np
from jax import lax
from jax.experimental import pallas as pl
from jax.experimental.pallas import tpu as pltpu
from jax.sharding import PartitionSpec as P

MESH = pl.DeviceIdType.MESH
BF = jnp.bfloat16
F32 = jnp.float32

N = 1024
M = 64
S = 64
XL = 16
J = 8
CL = 24
PL = 2
OB = 8
H = CL * XL


def _bf(a):
    return np.asarray(a, np.float32).astype(jnp.bfloat16)


def _split(a):
    hi = _bf(a)
    return hi, _bf(np.asarray(a, np.float64) - hi.astype(np.float64))


@functools.cache
def tables():
    y = np.arange(N)
    ky = np.arange(M)
    ang = 2 * np.pi * ((ky[:, None] * y[None, :]) % N) / N
    sc = 1 / math.sqrt(N)
    yt = _bf(np.stack([np.cos(ang) * sc, -np.sin(ang) * sc], 1).reshape(2 * M, N))
    wgt = np.where(ky == 0, 1.0, 2.0)[:, None]
    g = np.stack([wgt * np.cos(ang) * sc, -wgt * np.sin(ang) * sc], 1).reshape(2 * M, N)
    g2 = np.concatenate(_split(g * math.sqrt(0.5)), 0)

    k = np.arange(M)
    s = np.arange(S)
    ph = 2 * np.pi * ((k[:, None] * s[None, :]) % S) / S
    c, d = np.cos(ph) * sc, np.sin(ph) * sc
    dm = np.zeros((2, M, S, 2))
    dm[0, :, :, 0], dm[0, :, :, 1] = c, d
    dm[1, :, :, 0], dm[1, :, :, 1] = -d, c
    d2 = np.concatenate(_split(dm.reshape(2 * M, 2 * S)), 1)

    f = np.where(k < M // 2, k, k - M)
    tw = 2 * np.pi * f[:, None] * np.arange(XL)[None, :] / N
    tct = np.tile(np.cos(tw), (1, 8))
    tst = np.tile(np.sin(tw), (1, 8))

    bt = np.zeros((CL, CL, XL), np.float32)
    ex = np.zeros((2, 2, CL, 2, CL, XL), np.float32)
    for o in range(CL):
        bt[o, o] = 1
        for w in range(2):
            ex[:, w, o, w, o, :] = 1
    bt = _bf(bt.reshape(CL, H))
    ex = _bf(ex.reshape(4 * CL, 2 * H))

    e = np.zeros((S, 2, 2, 2, M))
    for ab in range(2):
        for r in range(2):
            val = np.exp(1j * ph.T) * (1j ** (r + ab)) * sc
            e[:, 0, ab, r] = val.real
            e[:, 1, ab, r] = val.imag
    ehi, elo = _split(e.reshape(2 * S, 256))
    ee = np.concatenate([ehi, elo], 0)
    tf = np.concatenate([tct, tst], 0).astype(np.float32)
    return dict(yt=yt, g2=g2, d2=d2, tf=tf, bt=bt, ex=ex, ee=ee)


def split(v):
    hi = v.astype(BF)
    return hi, (v - hi.astype(F32)).astype(BF)


def dot(a, b):
    return jnp.dot(a, b, preferred_element_type=F32)


def dot_nt(a, b):
    return lax.dot_general(a, b, (((1,), (1,)), ((), ())), preferred_element_type=F32)


NAMES = ("yt", "d2", "tf", "bt", "ex", "ee")


def exchange_kernel(*refs):
    nt = len(NAMES)
    field_h, w_h, bias_h = refs[:3]
    tabs_h = refs[3:3 + nt]
    g2_h, half_h, back_h, g2_o, bias_o = refs[3 + nt:8 + nt]
    fbuf, wbuf, bias_s = refs[8 + nt:11 + nt]
    tabs = dict(zip(NAMES, refs[11 + nt:11 + 2 * nt]))
    (send1, recv1, ags, agr, send2, recv2, obuf,
     g2, bias_v, in_sem, loc_sem, s1, r1, sa, ra, s2, r2, out_sem) = refs[11 + 2 * nt:]

    me = lax.axis_index("gx")
    mc = lax.axis_index("col")

    first = [pltpu.make_async_copy(tabs_h[0], tabs["yt"], in_sem.at[0])]
    first += [pltpu.make_async_copy(field_h.at[:, p], fbuf.at[p], in_sem.at[1 + p]) for p in range(PL)]
    rest = [pltpu.make_async_copy(h, tabs[n], in_sem.at[5 + i])
            for i, (h, n) in enumerate(zip(tabs_h[1:], NAMES[1:]))]
    rest += [pltpu.make_async_copy(w_h, wbuf, in_sem.at[3]),
             pltpu.make_async_copy(bias_h, bias_s, in_sem.at[4]),
             pltpu.make_async_copy(g2_h, g2, in_sem.at[10])]
    for c in first:
        c.start()

    barrier = pltpu.get_barrier_semaphore()

    def hello(axis, t):
        pl.semaphore_signal(barrier, inc=1, device_id={axis: t}, device_id_type=MESH)

    def around(go):
        go(lax.rem(me + S // 2, S))

        def step(i, _):
            for n in range(3):
                d = 3 * i + n + 1
                go(lax.rem(me + S // 2 - d, S))
                go(lax.rem(me + S // 2 + d, S))
            return 0

        lax.fori_loop(0, 10, step, 0)
        go(lax.rem(me + 1, S))
        go(lax.rem(me + S - 1, S))

    def greet_col(i, _):
        hello("col", lax.rem(mc + i, J))
        return 0

    around(lambda t: hello("gx", t))
    lax.fori_loop(1, J, greet_col, 0)
    for c in rest:
        c.start()
    first[0].wait()
    for p in range(PL):
        first[1 + p].wait()
        h = dot_nt(tabs["yt"][...], fbuf[p].reshape(H, N))
        send1[p] = h.astype(BF).reshape(S, 2, H)

    pl.semaphore_wait(barrier, S - 1 + J - 1)

    def message(t, send, recv, ssem, rsem):
        return pltpu.make_async_remote_copy(
            src_ref=send.at[t], dst_ref=recv.at[me], send_sem=ssem, recv_sem=rsem,
            device_id={"gx": t}, device_id_type=MESH)

    def exchange(*refs):
        own = pltpu.make_async_copy(refs[0].at[me], refs[1].at[me], loc_sem)
        own.start()
        around(lambda t: message(t, *refs).start())
        own.wait()

    def others(send, recv, ssem, rsem):
        every = pl.ds(0, S - 1)
        return pltpu.make_async_remote_copy(
            src_ref=send.at[every], dst_ref=recv.at[every], send_sem=ssem, recv_sem=rsem,
            device_id={"gx": lax.rem(me + 1, S)}, device_id_type=MESH)

    def arrive(*refs):
        others(*refs).wait_recv()

    def drain(*refs):
        others(*refs).wait_send()

    def port(send, recv, ssem, rsem, p):
        return send.at[p], recv.at[p], ssem.at[p], rsem.at[p]

    ports1 = [port(send1, recv1, s1, r1, p) for p in range(PL)]
    ports2 = [port(send2, recv2, s2, r2, p) for p in range(PL)]

    def columns(p):
        own = pltpu.make_async_copy(ags.at[p], agr.at[p, mc], loc_sem)
        own.start()

        def one(i, _):
            pltpu.make_async_remote_copy(
                src_ref=ags.at[p], dst_ref=agr.at[p, mc], send_sem=sa.at[p], recv_sem=ra.at[p],
                device_id={"col": lax.rem(mc + i, J)}, device_id_type=MESH).start()
            return 0

        lax.fori_loop(1, J, one, 0)
        own.wait()

    def column_bytes(p):
        every = agr.at[p, pl.ds(0, J - 1)]
        return pltpu.make_async_remote_copy(
            src_ref=every, dst_ref=every, send_sem=sa.at[p], recv_sem=ra.at[p],
            device_id={"col": lax.rem(mc + 1, J)}, device_id_type=MESH)

    for p in range(PL):
        exchange(*ports1[p])
    for c in rest:
        c.wait()

    tc = jnp.concatenate([tabs["tf"][0:M]] * 3, 1)
    ts = jnp.concatenate([tabs["tf"][M:2 * M]] * 3, 1)
    for p in range(PL):
        arrive(*ports1[p])
        got = recv1[p].reshape(2 * S, H)
        g = dot(tabs["d2"][...], jnp.concatenate([got, got], 0))
        gr, gi = g[:M], g[M:]
        hi, lo = split(jnp.concatenate([tc * gr + ts * gi, tc * gi - ts * gr], 0))
        bt = tabs["bt"][...]
        ags[p] = (dot_nt(bt, hi) + dot_nt(bt, lo)).astype(BF)
        columns(p)

    lane = lax.broadcasted_iota(jnp.int32, (2 * CL, 2 * M), 1) % M
    tc = jnp.concatenate([tc, tc], 0)
    ts = jnp.concatenate([ts, ts], 0)
    for p in range(PL):
        column_bytes(p).wait_recv()
        a = agr[p].reshape(J * CL, 2 * M)
        mixed = jnp.zeros((2 * CL, 2 * M), F32)
        for kg in range(8):
            z = dot(wbuf[384 * kg:384 * kg + 384, :], a)
            for i in range(8):
                mixed = jnp.where(lane == 8 * kg + i, z[48 * i:48 * i + 48], mixed)
        hi, lo = split(mixed)
        y = lax.dot_general(jnp.concatenate([hi, lo], 0), tabs["ex"][...], (((0,), (0,)), ((), ())),
                            preferred_element_type=F32)
        y0, y1 = y[:, :H], y[:, H:]
        hi, lo = split(jnp.concatenate([tc * y0 - ts * y1, tc * y1 + ts * y0], 0))
        ee = tabs["ee"]
        wide = dot(ee[:128], hi) + dot(ee[128:], hi) + dot(ee[:128], lo)
        send2[p] = wide.astype(BF).reshape(S, 2, H)
        exchange(*ports2[p])

    for p in range(PL):
        drain(*ports1[p])
        column_bytes(p).wait_send()
    for o in range(CL):
        bias_v[o] = jnp.full((XL, 128), bias_s[o] * math.sqrt(0.5), F32)
    puts = [pltpu.make_async_copy(g2, g2_o, out_sem.at[0]),
            pltpu.make_async_copy(bias_v, bias_o, out_sem.at[1])]
    for put in puts:
        put.start()
    arrive(*ports2[0])
    finish_plane(recv2[0], g2, bias_v, obuf)
    puts.append(pltpu.make_async_copy(obuf, half_h, out_sem.at[2]))
    puts[-1].start()
    for p in range(PL):
        drain(*ports2[p])
    for put in puts:
        put.wait()
    arrive(*ports2[1])
    put = pltpu.make_async_copy(recv2.at[1], back_h, out_sem.at[3])
    put.start()
    put.wait()


def finish_plane(msgs, g2, bias_v, obuf, done=None):
    got = msgs.reshape(2 * S, H)
    got = jnp.concatenate([got, got], 0)
    for n in range(CL // OB):
        v = lax.dot_general(got[:, 128 * n:128 * n + 128], g2[...], (((0,), (0,)), ((), ())),
                            preferred_element_type=F32)
        for i in range(OB):
            o = n * OB + i
            u = v[XL * i:XL * i + XL] + jnp.concatenate([bias_v[o]] * (N // 128), 1)
            t = u * math.sqrt(0.5)
            obuf[o] = (t + t * lax.erf(u)).astype(BF)
        if done is not None:
            done(n)


def finish_kernel(half_h, back_ref, g2_ref, bias_ref, out_h, obuf, sem):
    first = pltpu.make_async_copy(half_h, out_h.at[:, 0], sem.at[CL // OB])
    first.start()

    def put(n):
        rows = pl.ds(n * OB, OB)
        return pltpu.make_async_copy(obuf.at[rows], out_h.at[rows, 1], sem.at[n])

    finish_plane(back_ref[...], g2_ref, bias_ref, obuf, lambda n: put(n).start())
    for n in range(CL // OB):
        put(n).wait()
    first.wait()


def finish(half, back, g2, bias_v):
    return pl.pallas_call(
        finish_kernel,
        out_shape=jax.ShapeDtypeStruct((CL, PL, XL, N), BF),
        in_specs=[pl.BlockSpec(memory_space=pl.ANY)] + [pl.BlockSpec(memory_space=pltpu.VMEM)] * 3,
        out_specs=pl.BlockSpec(memory_space=pl.ANY),
        scratch_shapes=[pltpu.VMEM((CL, XL, N), BF), pltpu.SemaphoreType.DMA((CL // OB + 1,))],
        compiler_params=pltpu.CompilerParams(vmem_limit_bytes=24 * 2**20),
        name="finish",
    )(half, back, g2, bias_v)


def exchanges(field, w, bias, tabs):
    ops = [tabs[n] for n in NAMES]
    g2 = tabs["g2"]
    vm = [pltpu.VMEM((PL, CL, XL, N), BF), pltpu.VMEM((M * 2 * CL, J * CL), BF), pltpu.SMEM((CL,), F32)]
    vm += [pltpu.VMEM(t.shape, t.dtype) for t in ops]
    msg = pltpu.VMEM((PL, S, 2, H), BF)
    dma = pltpu.SemaphoreType.DMA
    return pl.pallas_call(
        exchange_kernel,
        out_shape=[jax.ShapeDtypeStruct((CL, XL, N), BF), jax.ShapeDtypeStruct((S, 2, H), BF),
                   jax.ShapeDtypeStruct(g2.shape, BF), jax.ShapeDtypeStruct((CL, XL, 128), F32)],
        in_specs=[pl.BlockSpec(memory_space=pl.ANY)] * (4 + len(ops)),
        out_specs=[pl.BlockSpec(memory_space=pl.ANY)] * 4,
        scratch_shapes=vm + [
            msg, msg, pltpu.VMEM((PL, CL, 2 * M), BF), pltpu.VMEM((PL, J, CL, 2 * M), BF), msg, msg,
            pltpu.VMEM((CL, XL, N), BF), pltpu.VMEM(g2.shape, BF), pltpu.VMEM((CL, XL, 128), F32),
            dma((5 + len(ops),)), dma,
            dma((PL,)), dma((PL,)), dma((PL,)), dma((PL,)), dma((PL,)), dma((PL,)), dma((4,))],
        compiler_params=pltpu.CompilerParams(
            collective_id=0, has_side_effects=True, vmem_limit_bytes=24 * 2**20),
        name="exchange",
    )(*[pltpu.with_memory_space_constraint(v, pltpu.HBM) for v in (field, w, bias, *ops, g2)])


def body(field, weights, bias):
    tabs = {n: jnp.asarray(t) for n, t in tables().items()}
    w = jnp.swapaxes(weights, 3, 4).reshape(M * 2 * CL, J * CL)
    return finish(*exchanges(field, w, bias, tabs))


def solution(mesh):
    placed = (P("col", None, "gx", None), P("gx", None, None, None, "col"), P("col"))
    return jax.shard_map(
        body, mesh=mesh, in_specs=placed, out_specs=P("col", None, "gx", None), check_vma=False
    )
```

```python
import functools
import math

import jax
import jax.numpy as jnp
import numpy as np
from jax import lax
from jax.experimental import pallas as pl
from jax.experimental.pallas import tpu as pltpu
from jax.sharding import PartitionSpec as P

MESH = pl.DeviceIdType.MESH
BF = jnp.bfloat16
F32 = jnp.float32

N = 1024
M = 64
S = 64
XL = 16
J = 8
CL = 24
PL = 2
OB = 8
H = CL * XL


def _bf(a):
    return np.asarray(a, np.float32).astype(jnp.bfloat16)


def _split(a):
    hi = _bf(a)
    return hi, _bf(np.asarray(a, np.float64) - hi.astype(np.float64))


@functools.cache
def tables():
    y = np.arange(N)
    ky = np.arange(M)
    ang = 2 * np.pi * ((ky[:, None] * y[None, :]) % N) / N
    sc = 1 / math.sqrt(N)
    yt = _bf(np.stack([np.cos(ang) * sc, -np.sin(ang) * sc], 1).reshape(2 * M, N))
    wgt = np.where(ky == 0, 1.0, 2.0)[:, None]
    g = np.stack([wgt * np.cos(ang) * sc, -wgt * np.sin(ang) * sc], 1).reshape(2 * M, N)
    g2 = np.concatenate(_split(g * math.sqrt(0.5)), 0)

    k = np.arange(M)
    s = np.arange(S)
    ph = 2 * np.pi * ((k[:, None] * s[None, :]) % S) / S
    c, d = np.cos(ph) * sc, np.sin(ph) * sc
    dm = np.zeros((2, M, S, 2))
    dm[0, :, :, 0], dm[0, :, :, 1] = c, d
    dm[1, :, :, 0], dm[1, :, :, 1] = -d, c
    d2 = np.concatenate(_split(dm.reshape(2 * M, 2 * S)), 1)

    f = np.where(k < M // 2, k, k - M)
    tw = 2 * np.pi * f[:, None] * np.arange(XL)[None, :] / N
    tct = np.tile(np.cos(tw), (1, 8))
    tst = np.tile(np.sin(tw), (1, 8))

    bt = np.zeros((CL, CL, XL), np.float32)
    ex = np.zeros((2, 2, CL, 2, CL, XL), np.float32)
    for o in range(CL):
        bt[o, o] = 1
        for w in range(2):
            ex[:, w, o, w, o, :] = 1
    bt = _bf(bt.reshape(CL, H))
    ex = _bf(ex.reshape(4 * CL, 2 * H))

    e = np.zeros((S, 2, 2, 2, M))
    for ab in range(2):
        for r in range(2):
            val = np.exp(1j * ph.T) * (1j ** (r + ab)) * sc
            e[:, 0, ab, r] = val.real
            e[:, 1, ab, r] = val.imag
    ehi, elo = _split(e.reshape(2 * S, 256))
    ee = np.concatenate([ehi, elo], 0)
    tf = np.concatenate([tct, tst], 0).astype(np.float32)
    return dict(yt=yt, g2=g2, d2=d2, tf=tf, bt=bt, ex=ex, ee=ee)


def split(v):
    hi = v.astype(BF)
    return hi, (v - hi.astype(F32)).astype(BF)


def dot(a, b):
    return jnp.dot(a, b, preferred_element_type=F32)


def dot_nt(a, b):
    return lax.dot_general(a, b, (((1,), (1,)), ((), ())), preferred_element_type=F32)


NAMES = ("yt", "d2", "tf", "bt", "ex", "ee")


def exchange_kernel(*refs):
    nt = len(NAMES)
    field_h, w_h, bias_h = refs[:3]
    tabs_h = refs[3:3 + nt]
    g2_h, half_h, back_h, g2_o, bias_o = refs[3 + nt:8 + nt]
    fbuf, wbuf, bias_s = refs[8 + nt:11 + nt]
    tabs = dict(zip(NAMES, refs[11 + nt:11 + 2 * nt]))
    (send1, recv1, ags, agr, send2, recv2, obuf,
     g2, bias_v, in_sem, loc_sem, s1, r1, sa, ra, s2, r2, out_sem) = refs[11 + 2 * nt:]

    me = lax.axis_index("gx")
    mc = lax.axis_index("col")

    first = [pltpu.make_async_copy(tabs_h[0], tabs["yt"], in_sem.at[0])]
    first += [pltpu.make_async_copy(field_h.at[:, p], fbuf.at[p], in_sem.at[1 + p]) for p in range(PL)]
    rest = [pltpu.make_async_copy(h, tabs[n], in_sem.at[5 + i])
            for i, (h, n) in enumerate(zip(tabs_h[1:], NAMES[1:]))]
    rest += [pltpu.make_async_copy(w_h, wbuf, in_sem.at[3]),
             pltpu.make_async_copy(bias_h, bias_s, in_sem.at[4]),
             pltpu.make_async_copy(g2_h, g2, in_sem.at[10])]
    for c in first:
        c.start()

    barrier = pltpu.get_barrier_semaphore()

    def hello(axis, t):
        pl.semaphore_signal(barrier, inc=1, device_id={axis: t}, device_id_type=MESH)

    def around(go):
        go(lax.rem(me + S // 2, S))

        def step(i, _):
            for n in range(3):
                d = 3 * i + n + 1
                go(lax.rem(me + S // 2 - d, S))
                go(lax.rem(me + S // 2 + d, S))
            return 0

        lax.fori_loop(0, 10, step, 0)
        go(lax.rem(me + 1, S))
        go(lax.rem(me + S - 1, S))

    def greet_col(i, _):
        hello("col", lax.rem(mc + i, J))
        return 0

    around(lambda t: hello("gx", t))
    lax.fori_loop(1, J, greet_col, 0)
    for c in rest:
        c.start()
    first[0].wait()
    for p in range(PL):
        first[1 + p].wait()
        h = dot_nt(tabs["yt"][...], fbuf[p].reshape(H, N))
        send1[p] = h.astype(BF).reshape(S, 2, H)

    pl.semaphore_wait(barrier, S - 1 + J - 1)

    def message(t, send, recv, ssem, rsem):
        return pltpu.make_async_remote_copy(
            src_ref=send.at[t], dst_ref=recv.at[me], send_sem=ssem, recv_sem=rsem,
            device_id={"gx": t}, device_id_type=MESH)

    def exchange(*refs):
        own = pltpu.make_async_copy(refs[0].at[me], refs[1].at[me], loc_sem)
        own.start()
        around(lambda t: message(t, *refs).start())
        own.wait()

    def others(send, recv, ssem, rsem):
        every = pl.ds(0, S - 1)
        return pltpu.make_async_remote_copy(
            src_ref=send.at[every], dst_ref=recv.at[every], send_sem=ssem, recv_sem=rsem,
            device_id={"gx": lax.rem(me + 1, S)}, device_id_type=MESH)

    def arrive(*refs):
        others(*refs).wait_recv()

    def drain(*refs):
        others(*refs).wait_send()

    def port(send, recv, ssem, rsem, p):
        return send.at[p], recv.at[p], ssem.at[p], rsem.at[p]

    ports1 = [port(send1, recv1, s1, r1, p) for p in range(PL)]
    ports2 = [(send2.at[p], land, s2.at[p], r2.at[p]) for p, land in enumerate((recv2, back_h))]

    def columns(p):
        own = pltpu.make_async_copy(ags.at[p], agr.at[p, mc], loc_sem)
        own.start()

        def one(i, _):
            pltpu.make_async_remote_copy(
                src_ref=ags.at[p], dst_ref=agr.at[p, mc], send_sem=sa.at[p], recv_sem=ra.at[p],
                device_id={"col": lax.rem(mc + i, J)}, device_id_type=MESH).start()
            return 0

        lax.fori_loop(1, J, one, 0)
        own.wait()

    def column_bytes(p):
        every = agr.at[p, pl.ds(0, J - 1)]
        return pltpu.make_async_remote_copy(
            src_ref=every, dst_ref=every, send_sem=sa.at[p], recv_sem=ra.at[p],
            device_id={"col": lax.rem(mc + 1, J)}, device_id_type=MESH)

    for p in range(PL):
        exchange(*ports1[p])
    for c in rest:
        c.wait()

    tc = jnp.concatenate([tabs["tf"][0:M]] * 3, 1)
    ts = jnp.concatenate([tabs["tf"][M:2 * M]] * 3, 1)
    for p in range(PL):
        arrive(*ports1[p])
        got = recv1[p].reshape(2 * S, H)
        g = dot(tabs["d2"][...], jnp.concatenate([got, got], 0))
        gr, gi = g[:M], g[M:]
        hi, lo = split(jnp.concatenate([tc * gr + ts * gi, tc * gi - ts * gr], 0))
        bt = tabs["bt"][...]
        ags[p] = (dot_nt(bt, hi) + dot_nt(bt, lo)).astype(BF)
        columns(p)

    lane = lax.broadcasted_iota(jnp.int32, (2 * CL, 2 * M), 1) % M
    tc = jnp.concatenate([tc, tc], 0)
    ts = jnp.concatenate([ts, ts], 0)
    for p in range(PL):
        column_bytes(p).wait_recv()
        a = agr[p].reshape(J * CL, 2 * M)
        mixed = jnp.zeros((2 * CL, 2 * M), F32)
        for kg in range(8):
            z = dot(wbuf[384 * kg:384 * kg + 384, :], a)
            for i in range(8):
                mixed = jnp.where(lane == 8 * kg + i, z[48 * i:48 * i + 48], mixed)
        hi, lo = split(mixed)
        y = lax.dot_general(jnp.concatenate([hi, lo], 0), tabs["ex"][...], (((0,), (0,)), ((), ())),
                            preferred_element_type=F32)
        y0, y1 = y[:, :H], y[:, H:]
        hi, lo = split(jnp.concatenate([tc * y0 - ts * y1, tc * y1 + ts * y0], 0))
        ee = tabs["ee"]
        wide = dot(ee[:128], hi) + dot(ee[128:], hi) + dot(ee[:128], lo)
        send2[p] = wide.astype(BF).reshape(S, 2, H)
        exchange(*ports2[p])

    for p in range(PL):
        drain(*ports1[p])
        column_bytes(p).wait_send()
    for o in range(CL):
        bias_v[o] = jnp.full((XL, 128), bias_s[o] * math.sqrt(0.5), F32)
    puts = [pltpu.make_async_copy(g2, g2_o, out_sem.at[0]),
            pltpu.make_async_copy(bias_v, bias_o, out_sem.at[1])]
    for put in puts:
        put.start()
    arrive(*ports2[0])
    finish_plane(recv2[...], g2, bias_v, obuf)
    puts.append(pltpu.make_async_copy(obuf, half_h, out_sem.at[2]))
    puts[-1].start()
    for p in range(PL):
        drain(*ports2[p])
    for put in puts:
        put.wait()
    arrive(*ports2[1])


def finish_plane(msgs, g2, bias_v, obuf, done=None):
    got = msgs.reshape(2 * S, H)
    got = jnp.concatenate([got, got], 0)
    for n in range(CL // OB):
        v = lax.dot_general(got[:, 128 * n:128 * n + 128], g2[...], (((0,), (0,)), ((), ())),
                            preferred_element_type=F32)
        for i in range(OB):
            o = n * OB + i
            u = v[XL * i:XL * i + XL] + jnp.concatenate([bias_v[o]] * (N // 128), 1)
            t = u * math.sqrt(0.5)
            obuf[o] = (t + t * lax.erf(u)).astype(BF)
        if done is not None:
            done(n)


def finish_kernel(half_h, back_ref, g2_ref, bias_ref, out_h, obuf, sem):
    first = pltpu.make_async_copy(half_h, out_h.at[:, 0], sem.at[CL // OB])
    first.start()

    def put(n):
        rows = pl.ds(n * OB, OB)
        return pltpu.make_async_copy(obuf.at[rows], out_h.at[rows, 1], sem.at[n])

    finish_plane(back_ref[...], g2_ref, bias_ref, obuf, lambda n: put(n).start())
    for n in range(CL // OB):
        put(n).wait()
    first.wait()


def finish(half, back, g2, bias_v):
    return pl.pallas_call(
        finish_kernel,
        out_shape=jax.ShapeDtypeStruct((CL, PL, XL, N), BF),
        in_specs=[pl.BlockSpec(memory_space=pl.ANY)] + [pl.BlockSpec(memory_space=pltpu.VMEM)] * 3,
        out_specs=pl.BlockSpec(memory_space=pl.ANY),
        scratch_shapes=[pltpu.VMEM((CL, XL, N), BF), pltpu.SemaphoreType.DMA((CL // OB + 1,))],
        compiler_params=pltpu.CompilerParams(vmem_limit_bytes=24 * 2**20),
        name="finish",
    )(half, back, g2, bias_v)


def exchanges(field, w, bias, tabs):
    ops = [tabs[n] for n in NAMES]
    g2 = tabs["g2"]
    vm = [pltpu.VMEM((PL, CL, XL, N), BF), pltpu.VMEM((M * 2 * CL, J * CL), BF), pltpu.SMEM((CL,), F32)]
    vm += [pltpu.VMEM(t.shape, t.dtype) for t in ops]
    msg = pltpu.VMEM((PL, S, 2, H), BF)
    dma = pltpu.SemaphoreType.DMA
    return pl.pallas_call(
        exchange_kernel,
        out_shape=[jax.ShapeDtypeStruct((CL, XL, N), BF), jax.ShapeDtypeStruct((S, 2, H), BF),
                   jax.ShapeDtypeStruct(g2.shape, BF), jax.ShapeDtypeStruct((CL, XL, 128), F32)],
        in_specs=[pl.BlockSpec(memory_space=pl.ANY)] * (4 + len(ops)),
        out_specs=[pl.BlockSpec(memory_space=pl.ANY)] * 4,
        scratch_shapes=vm + [
            msg, msg, pltpu.VMEM((PL, CL, 2 * M), BF), pltpu.VMEM((PL, J, CL, 2 * M), BF), msg, pltpu.VMEM((S, 2, H), BF),
            pltpu.VMEM((CL, XL, N), BF), pltpu.VMEM(g2.shape, BF), pltpu.VMEM((CL, XL, 128), F32),
            dma((5 + len(ops),)), dma,
            dma((PL,)), dma((PL,)), dma((PL,)), dma((PL,)), dma((PL,)), dma((PL,)), dma((3,))],
        compiler_params=pltpu.CompilerParams(
            collective_id=0, has_side_effects=True, vmem_limit_bytes=24 * 2**20),
        name="exchange",
    )(*[pltpu.with_memory_space_constraint(v, pltpu.HBM) for v in (field, w, bias, *ops, g2)])


def body(field, weights, bias):
    tabs = {n: jnp.asarray(t) for n, t in tables().items()}
    w = jnp.swapaxes(weights, 3, 4).reshape(M * 2 * CL, J * CL)
    return finish(*exchanges(field, w, bias, tabs))


def solution(mesh):
    placed = (P("col", None, "gx", None), P("gx", None, None, None, "col"), P("col"))
    return jax.shard_map(
        body, mesh=mesh, in_specs=placed, out_specs=P("col", None, "gx", None), check_vma=False
    )
```

```python
import functools
import math

import jax
import jax.numpy as jnp
import numpy as np
from jax import lax
from jax.experimental import pallas as pl
from jax.experimental.pallas import tpu as pltpu
from jax.sharding import PartitionSpec as P

MESH = pl.DeviceIdType.MESH
BF = jnp.bfloat16
F32 = jnp.float32

N = 1024
M = 64
S = 64
XL = 16
J = 8
CL = 24
PL = 2
OB = 8
H = CL * XL


def _bf(a):
    return np.asarray(a, np.float32).astype(jnp.bfloat16)


def _split(a):
    hi = _bf(a)
    return hi, _bf(np.asarray(a, np.float64) - hi.astype(np.float64))


@functools.cache
def tables():
    y = np.arange(N)
    ky = np.arange(M)
    ang = 2 * np.pi * ((ky[:, None] * y[None, :]) % N) / N
    sc = 1 / math.sqrt(N)
    yt = _bf(np.stack([np.cos(ang) * sc, -np.sin(ang) * sc], 1).reshape(2 * M, N))
    wgt = np.where(ky == 0, 1.0, 2.0)[:, None]
    g = np.stack([wgt * np.cos(ang) * sc, -wgt * np.sin(ang) * sc], 1).reshape(2 * M, N)
    g2 = np.concatenate(_split(g * math.sqrt(0.5)), 0)

    k = np.arange(M)
    s = np.arange(S)
    ph = 2 * np.pi * ((k[:, None] * s[None, :]) % S) / S
    c, d = np.cos(ph) * sc, np.sin(ph) * sc
    dm = np.zeros((2, M, S, 2))
    dm[0, :, :, 0], dm[0, :, :, 1] = c, d
    dm[1, :, :, 0], dm[1, :, :, 1] = -d, c
    d2 = np.concatenate(_split(dm.reshape(2 * M, 2 * S)), 1)

    f = np.where(k < M // 2, k, k - M)
    tw = 2 * np.pi * f[:, None] * np.arange(XL)[None, :] / N
    tct = np.tile(np.cos(tw), (1, 8))
    tst = np.tile(np.sin(tw), (1, 8))

    bt = np.zeros((CL, CL, XL), np.float32)
    ex = np.zeros((2, 2, CL, 2, CL, XL), np.float32)
    for o in range(CL):
        bt[o, o] = 1
        for w in range(2):
            ex[:, w, o, w, o, :] = 1
    bt = _bf(bt.reshape(CL, H))
    ex = _bf(ex.reshape(4 * CL, 2 * H))

    e = np.zeros((S, 2, 2, 2, M))
    for ab in range(2):
        for r in range(2):
            val = np.exp(1j * ph.T) * (1j ** (r + ab)) * sc
            e[:, 0, ab, r] = val.real
            e[:, 1, ab, r] = val.imag
    ehi, elo = _split(e.reshape(2 * S, 256))
    ee = np.concatenate([ehi, elo], 0)
    tf = np.concatenate([tct, tst], 0).astype(np.float32)
    return dict(yt=yt, g2=g2, d2=d2, tf=tf, bt=bt, ex=ex, ee=ee)


def split(v):
    hi = v.astype(BF)
    return hi, (v - hi.astype(F32)).astype(BF)


def dot(a, b):
    return jnp.dot(a, b, preferred_element_type=F32)


def dot_nt(a, b):
    return lax.dot_general(a, b, (((1,), (1,)), ((), ())), preferred_element_type=F32)


NAMES = ("yt", "d2", "tf", "bt", "ex", "ee")


def exchange_kernel(*refs):
    nt = len(NAMES)
    field_h, w_h, bias_h = refs[:3]
    tabs_h = refs[3:3 + nt]
    g2_h, half_h, back_h, g2_o, bias_o = refs[3 + nt:8 + nt]
    fbuf, wbuf, bias_s = refs[8 + nt:11 + nt]
    tabs = dict(zip(NAMES, refs[11 + nt:11 + 2 * nt]))
    (send1, recv1, ags, agr, send2, recv2, obuf,
     g2, bias_v, in_sem, loc_sem, s1, r1, sa, ra, s2, r2, out_sem, own_sem) = refs[11 + 2 * nt:]

    me = lax.axis_index("gx")
    mc = lax.axis_index("col")

    first = [pltpu.make_async_copy(tabs_h[0], tabs["yt"], in_sem.at[0])]
    first += [pltpu.make_async_copy(field_h.at[:, p], fbuf.at[p], in_sem.at[1 + p]) for p in range(PL)]
    rest = [pltpu.make_async_copy(h, tabs[n], in_sem.at[5 + i])
            for i, (h, n) in enumerate(zip(tabs_h[1:], NAMES[1:]))]
    rest += [pltpu.make_async_copy(w_h, wbuf, in_sem.at[3]),
             pltpu.make_async_copy(bias_h, bias_s, in_sem.at[4]),
             pltpu.make_async_copy(g2_h, g2, in_sem.at[10])]
    for c in first:
        c.start()

    barrier = pltpu.get_barrier_semaphore()

    def hello(axis, t):
        pl.semaphore_signal(barrier, inc=1, device_id={axis: t}, device_id_type=MESH)

    def around(go):
        go(lax.rem(me + S // 2, S))

        def step(i, _):
            for n in range(3):
                d = 3 * i + n + 1
                go(lax.rem(me + S // 2 - d, S))
                go(lax.rem(me + S // 2 + d, S))
            return 0

        lax.fori_loop(0, 10, step, 0)
        go(lax.rem(me + 1, S))
        go(lax.rem(me + S - 1, S))

    def greet_col(i, _):
        hello("col", lax.rem(mc + i, J))
        return 0

    around(lambda t: hello("gx", t))
    lax.fori_loop(1, J, greet_col, 0)
    for c in rest:
        c.start()
    first[0].wait()
    for p in range(PL):
        first[1 + p].wait()
        h = dot_nt(tabs["yt"][...], fbuf[p].reshape(H, N))
        send1[p] = h.astype(BF).reshape(S, 2, H)

    pl.semaphore_wait(barrier, S - 1 + J - 1)

    def message(t, send, recv, ssem, rsem):
        return pltpu.make_async_remote_copy(
            src_ref=send.at[t], dst_ref=recv.at[me], send_sem=ssem, recv_sem=rsem,
            device_id={"gx": t}, device_id_type=MESH)

    def exchange(*refs):
        own = pltpu.make_async_copy(refs[0].at[me], refs[1].at[me], loc_sem)
        own.start()
        around(lambda t: message(t, *refs).start())
        own.wait()

    def others(send, recv, ssem, rsem):
        every = pl.ds(0, S - 1)
        return pltpu.make_async_remote_copy(
            src_ref=send.at[every], dst_ref=recv.at[every], send_sem=ssem, recv_sem=rsem,
            device_id={"gx": lax.rem(me + 1, S)}, device_id_type=MESH)

    def arrive(*refs):
        others(*refs).wait_recv()

    def drain(*refs):
        others(*refs).wait_send()

    def port(send, recv, ssem, rsem, p):
        return send.at[p], recv.at[p], ssem.at[p], rsem.at[p]

    ports1 = [port(send1, recv1, s1, r1, p) for p in range(PL)]
    ports2 = [(send2.at[p], land, s2.at[p], r2.at[p]) for p, land in enumerate((recv2, back_h))]

    def columns(p):
        own = pltpu.make_async_copy(ags.at[p], agr.at[p, mc], own_sem.at[p])
        own.start()

        def to(t):
            pltpu.make_async_remote_copy(
                src_ref=ags.at[p], dst_ref=agr.at[p, mc], send_sem=sa.at[p], recv_sem=ra.at[p],
                device_id={"col": lax.rem(t, J)}, device_id_type=MESH).start()

        to(mc + J // 2)

        def pair(i, _):
            to(mc + J // 2 - i)
            to(mc + J // 2 + i)
            return 0

        lax.fori_loop(1, J // 2, pair, 0)

    def column_bytes(p):
        every = agr.at[p, pl.ds(0, J - 1)]
        return pltpu.make_async_remote_copy(
            src_ref=every, dst_ref=every, send_sem=sa.at[p], recv_sem=ra.at[p],
            device_id={"col": lax.rem(mc + 1, J)}, device_id_type=MESH)

    for p in range(PL):
        exchange(*ports1[p])
    for c in rest:
        c.wait()

    tc = jnp.concatenate([tabs["tf"][0:M]] * 3, 1)
    ts = jnp.concatenate([tabs["tf"][M:2 * M]] * 3, 1)
    for p in range(PL):
        arrive(*ports1[p])
        got = recv1[p].reshape(2 * S, H)
        g = dot(tabs["d2"][...], jnp.concatenate([got, got], 0))
        gr, gi = g[:M], g[M:]
        hi, lo = split(jnp.concatenate([tc * gr + ts * gi, tc * gi - ts * gr], 0))
        bt = tabs["bt"][...]
        ags[p] = (dot_nt(bt, hi) + dot_nt(bt, lo)).astype(BF)
        columns(p)

    lane = lax.broadcasted_iota(jnp.int32, (2 * CL, 2 * M), 1) % M
    tc = jnp.concatenate([tc, tc], 0)
    ts = jnp.concatenate([ts, ts], 0)
    for p in range(PL):
        column_bytes(p).wait_recv()
        pltpu.make_async_copy(ags.at[p], agr.at[p, mc], own_sem.at[p]).wait()
        a = agr[p].reshape(J * CL, 2 * M)
        mixed = jnp.zeros((2 * CL, 2 * M), F32)
        for kg in range(8):
            z = dot(wbuf[384 * kg:384 * kg + 384, :], a)
            for i in range(8):
                mixed = jnp.where(lane == 8 * kg + i, z[48 * i:48 * i + 48], mixed)
        hi, lo = split(mixed)
        y = lax.dot_general(jnp.concatenate([hi, lo], 0), tabs["ex"][...], (((0,), (0,)), ((), ())),
                            preferred_element_type=F32)
        y0, y1 = y[:, :H], y[:, H:]
        hi, lo = split(jnp.concatenate([tc * y0 - ts * y1, tc * y1 + ts * y0], 0))
        ee = tabs["ee"]
        wide = dot(ee[:128], hi) + dot(ee[128:], hi) + dot(ee[:128], lo)
        send2[p] = wide.astype(BF).reshape(S, 2, H)
        exchange(*ports2[p])

    for p in range(PL):
        drain(*ports1[p])
        column_bytes(p).wait_send()
    for o in range(CL):
        bias_v[o] = jnp.full((XL, 128), bias_s[o] * math.sqrt(0.5), F32)
    puts = [pltpu.make_async_copy(g2, g2_o, out_sem.at[0]),
            pltpu.make_async_copy(bias_v, bias_o, out_sem.at[1])]
    for put in puts:
        put.start()
    arrive(*ports2[0])
    finish_plane(recv2[...], g2, bias_v, obuf)
    puts.append(pltpu.make_async_copy(obuf, half_h, out_sem.at[2]))
    puts[-1].start()
    for p in range(PL):
        drain(*ports2[p])
    for put in puts:
        put.wait()
    arrive(*ports2[1])


def finish_plane(msgs, g2, bias_v, obuf, done=None):
    got = msgs.reshape(2 * S, H)
    got = jnp.concatenate([got, got], 0)
    for n in range(CL // OB):
        v = lax.dot_general(got[:, 128 * n:128 * n + 128], g2[...], (((0,), (0,)), ((), ())),
                            preferred_element_type=F32)
        for i in range(OB):
            o = n * OB + i
            u = v[XL * i:XL * i + XL] + jnp.concatenate([bias_v[o]] * (N // 128), 1)
            t = u * math.sqrt(0.5)
            obuf[o] = (t + t * lax.erf(u)).astype(BF)
        if done is not None:
            done(n)


def finish_kernel(half_h, back_ref, g2_ref, bias_ref, out_h, obuf, sem):
    first = pltpu.make_async_copy(half_h, out_h.at[:, 0], sem.at[CL // OB])
    first.start()

    def put(n):
        rows = pl.ds(n * OB, OB)
        return pltpu.make_async_copy(obuf.at[rows], out_h.at[rows, 1], sem.at[n])

    finish_plane(back_ref[...], g2_ref, bias_ref, obuf, lambda n: put(n).start())
    for n in range(CL // OB):
        put(n).wait()
    first.wait()


def finish(half, back, g2, bias_v):
    return pl.pallas_call(
        finish_kernel,
        out_shape=jax.ShapeDtypeStruct((CL, PL, XL, N), BF),
        in_specs=[pl.BlockSpec(memory_space=pl.ANY)] + [pl.BlockSpec(memory_space=pltpu.VMEM)] * 3,
        out_specs=pl.BlockSpec(memory_space=pl.ANY),
        scratch_shapes=[pltpu.VMEM((CL, XL, N), BF), pltpu.SemaphoreType.DMA((CL // OB + 1,))],
        compiler_params=pltpu.CompilerParams(vmem_limit_bytes=24 * 2**20),
        name="finish",
    )(half, back, g2, bias_v)


def exchanges(field, w, bias, tabs):
    ops = [tabs[n] for n in NAMES]
    g2 = tabs["g2"]
    vm = [pltpu.VMEM((PL, CL, XL, N), BF), pltpu.VMEM((M * 2 * CL, J * CL), BF), pltpu.SMEM((CL,), F32)]
    vm += [pltpu.VMEM(t.shape, t.dtype) for t in ops]
    msg = pltpu.VMEM((PL, S, 2, H), BF)
    dma = pltpu.SemaphoreType.DMA
    return pl.pallas_call(
        exchange_kernel,
        out_shape=[jax.ShapeDtypeStruct((CL, XL, N), BF), jax.ShapeDtypeStruct((S, 2, H), BF),
                   jax.ShapeDtypeStruct(g2.shape, BF), jax.ShapeDtypeStruct((CL, XL, 128), F32)],
        in_specs=[pl.BlockSpec(memory_space=pl.ANY)] * (4 + len(ops)),
        out_specs=[pl.BlockSpec(memory_space=pl.ANY)] * 4,
        scratch_shapes=vm + [
            msg, msg, pltpu.VMEM((PL, CL, 2 * M), BF), pltpu.VMEM((PL, J, CL, 2 * M), BF), msg, pltpu.VMEM((S, 2, H), BF),
            pltpu.VMEM((CL, XL, N), BF), pltpu.VMEM(g2.shape, BF), pltpu.VMEM((CL, XL, 128), F32),
            dma((5 + len(ops),)), dma,
            dma((PL,)), dma((PL,)), dma((PL,)), dma((PL,)), dma((PL,)), dma((PL,)), dma((3,)), dma((PL,))],
        compiler_params=pltpu.CompilerParams(
            collective_id=0, has_side_effects=True, vmem_limit_bytes=24 * 2**20),
        name="exchange",
    )(*[pltpu.with_memory_space_constraint(v, pltpu.HBM) for v in (field, w, bias, *ops, g2)])


def body(field, weights, bias):
    tabs = {n: jnp.asarray(t) for n, t in tables().items()}
    w = jnp.swapaxes(weights, 3, 4).reshape(M * 2 * CL, J * CL)
    return finish(*exchanges(field, w, bias, tabs))


def solution(mesh):
    placed = (P("col", None, "gx", None), P("gx", None, None, None, "col"), P("col"))
    return jax.shard_map(
        body, mesh=mesh, in_specs=placed, out_specs=P("col", None, "gx", None), check_vma=False
    )
```
